512 devices in a mesh: seq: 16 (over x, y_lo, core), head: 32 (over z, y_hi).
Axes of the slice: x: 4, y: 4 (y_hi: 2, y_lo: 2; y = y_hi * 2 + y_lo), z: 16, core: 2. Of those that a mesh axis runs over, the one named last changes fastest.
Arguments:
- queries: bfloat16 [65536, 4096], P(('seq', 'head')), may hold values from -56 to 56
- key_states: bfloat16 [65536, 1024], P(('seq', 'head')), may hold values from -6 to 6
- value_states: bfloat16 [65536, 1024], P(('seq', 'head')), may hold values from -6 to 6
- key_picks: int32 [128, 3], replicated, may hold values from 0 to 127, as said below
- positions: int32 [65536], P(('seq', 'head')), may hold values from 0 to 131070, as said below
Outputs:
- attended: bfloat16 [65536, 4096], P(('seq', 'head'))
The draws below stay inside these ranges and needn't reach their ends.
Inputs may be any that keep to these rules, and one draw needn't show every extreme that they name: `positions`: strictly increasing, the first is 0 and the last is 131070. `key_picks`: the 3 entries of a row are distinct. Entries at or above the row's own block number occur only where fewer than 3 earlier blocks may be picked, name blocks from the end of the sequence, and are dropped. Groups are runs of 8 blocks; of the blocks of one group, at most 3 are picked by query blocks of later groups, and some group has exactly 3 such blocks.
All inputs are finite; a program needn't handle non-finite values.
Results may differ from the reference program's by a relative error of at most 0.02.
Values may be sent and summed in bfloat16 or wider, within the bound.
A program may use at most 64 MiB of HBM per device.

```python
import math
import jax
import jax.numpy as jnp
from jax import lax

QH = 32
KVH = 8
HD = 128
BLOCK = 512
TOPK = 3
TOKENS = 65536
GB = 8
NB = 128
PUB = 3


def draw_positions(key, part):
    inner = jnp.arange(1, 2 * TOKENS - 2, dtype=jnp.int32)
    shuffled = jax.random.permutation(jax.random.fold_in(key, 11), inner)
    middle = jnp.sort(shuffled[:TOKENS - 2])
    first = jnp.zeros((1,), jnp.int32)
    last = jnp.full((1,), 2 * TOKENS - 2, jnp.int32)
    return jnp.concatenate([first, middle, last]).astype(jnp.int32)


def joint_states(key):
    states_keys = jax.random.truncated_normal(jax.random.fold_in(key, 21), -6.0, 6.0, (TOKENS, KVH, HD), jnp.float32)
    states_queries = jax.random.truncated_normal(jax.random.fold_in(key, 22), -6.0, 6.0, (TOKENS, QH, HD), jnp.float32)
    return (states_queries.reshape(TOKENS, QH * HD), states_keys.reshape(TOKENS, KVH * HD))


def draw_queries(key, part):
    return joint_states(key)[0].astype(jnp.bfloat16)


def draw_key_states(key, part):
    return joint_states(key)[1].astype(jnp.bfloat16)


def draw_key_picks(key, part):
    block_ids = jnp.arange(NB, dtype=jnp.int32)
    owner = block_ids // GB
    lottery = jax.random.randint(jax.random.fold_in(key, 31), (NB,), 0, 4096) * NB + block_ids
    same_group = owner[:, None] == owner[None, :]
    beaten = jnp.sum(same_group & (lottery[None, :] > lottery[:, None]), axis=1)
    is_public = beaten < PUB
    earlier = block_ids[None, :] < block_ids[:, None]
    allowed = earlier & (same_group | is_public[None, :])
    appeal = jax.random.randint(jax.random.fold_in(key, 32), (NB, NB), 0, 4096) // (1 + block_ids[None, :] * 4 // NB)
    fallback = jnp.where(earlier, -100000000 - block_ids[None, :], -1 - (NB - 1 - block_ids[None, :]) + 0 * block_ids[:, None])
    ranking = jnp.where(allowed, appeal * NB + block_ids[None, :], fallback)
    chosen = lax.top_k(ranking, TOPK)[1]
    return chosen.astype(jnp.int32)


def block_levels(stream_key, dims, pieces, low, top_value):
    def one(position, parts):
        heights = jax.random.uniform(jax.random.fold_in(jax.random.fold_in(stream_key, 6), position), (parts,), jnp.float32, low / len(pieces), top_value / len(pieces))
        return jnp.repeat(jnp.exp(heights), dims[position] // parts).reshape((-1,) + (1,) * (len(dims) - position - 1))

    factor_of = one(*pieces[0])
    for cut in pieces[1:]:
        factor_of = factor_of * one(*cut)
    return factor_of


def bell_draw(own_key, dims, spread, most, split=(), kind=jnp.bfloat16):
    factor_of = block_levels(own_key, dims, split, -0.22, 0.18) if split else 1.0
    drawn = jax.random.normal(own_key, dims, jnp.float32) * spread * factor_of
    return jnp.minimum(jnp.maximum(drawn, -most), most).astype(kind)


def setup_inputs(seed: int = 0) -> dict:
    streams_of = jax.random.split(jax.random.key(seed), 6)
    queries = draw_queries(jax.random.fold_in(streams_of[5], 71), 0)
    key_states = draw_key_states(jax.random.fold_in(streams_of[5], 71), 0)
    value_states = bell_draw(streams_of[2], (TOKENS, KVH * HD), 1.0, 6.0, ((0, 512),))
    key_picks = draw_key_picks(jax.random.fold_in(streams_of[5], 71), 0)
    positions = draw_positions(jax.random.fold_in(streams_of[5], 71), 0)
    return dict(queries=queries, key_states=key_states, value_states=value_states, key_picks=key_picks, positions=positions)


lowest = -1e+30

def frequency_table(columns):
    inverse = 1.0 / 500000.0 ** (jnp.arange(0, columns, 2, dtype=jnp.float32) / columns)
    wavelength = 2.0 * math.pi / inverse
    smooth = (8192.0 / wavelength - 1.0) / 3.0
    blended = (1.0 - smooth) * inverse / 8.0 + smooth * inverse
    return jnp.where(wavelength < 2048.0, inverse, jnp.where(wavelength > 8192.0, inverse / 8.0, blended))

def rotate(vectors, places):
    columns = vectors.shape[-1]
    halfway = columns // 2
    angles = places.astype(jnp.float32)[:, None] * frequency_table(columns).astype(jnp.float32)[None, :]
    cosine = jnp.cos(angles)[:, None, :]
    sine_of = jnp.sin(angles)[:, None, :]
    leading = vectors[..., :halfway]
    trailing = vectors[..., halfway:]
    return jnp.concatenate([leading * cosine - trailing * sine_of, trailing * cosine + leading * sine_of], axis=-1)

def block_partial(query_block, key_block, value_block, allowed):
    scaling = 1.0 / math.sqrt(query_block.shape[-1])
    scores = jnp.einsum('qkgd,skd->kgqs', query_block.astype(jnp.float32), key_block.astype(jnp.float32)) * scaling
    if allowed is not None:
        scores = jnp.where(allowed, scores, lowest)
    highest = lax.optimization_barrier(jnp.max(scores, axis=-1))
    weights = jnp.exp(scores - highest[..., None])
    summed = lax.optimization_barrier(jnp.sum(weights, axis=-1))
    rounded = lax.optimization_barrier(weights.astype(jnp.bfloat16))
    product = jnp.einsum('kgqs,skd->kgqd', rounded.astype(jnp.float32), value_block.astype(jnp.float32))
    return (highest, summed, product)

def combine_stats(former, latter):
    highest = jnp.maximum(former[0], latter[0])
    former_scale = jnp.exp(former[0] - highest)
    latter_scale = jnp.exp(latter[0] - highest)
    return (highest, former[1] * former_scale + latter[1] * latter_scale, former[2] * former_scale[..., None] + latter[2] * latter_scale[..., None])

def reference(queries, key_states, value_states, key_picks, positions):
    sharing = QH // KVH
    steps_in = jnp.arange(BLOCK, dtype=jnp.int32)
    causal = steps_in[:, None] >= steps_in[None, :]

    def take_rows(source, block_index, heads):
        return lax.dynamic_slice_in_dim(source, block_index * BLOCK, BLOCK, 0).reshape(BLOCK, heads, HD)

    def turned(source, block_index, heads):
        places = lax.dynamic_slice_in_dim(positions, block_index * BLOCK, BLOCK, 0)
        rotated = rotate(take_rows(source, block_index, heads).astype(jnp.float32), places).astype(jnp.bfloat16)
        return lax.optimization_barrier(rotated)

    def one_block(block_index):
        query_block = turned(queries, block_index, QH).reshape(BLOCK, KVH, sharing, HD)
        running = block_partial(query_block, turned(key_states, block_index, KVH), take_rows(value_states, block_index, KVH), causal)
        for pick_slot in range(TOPK):
            target = key_picks[block_index, pick_slot]
            in_use = target < block_index
            source_block = jnp.minimum(target, block_index)
            extra_part = block_partial(query_block, turned(key_states, source_block, KVH), take_rows(value_states, source_block, KVH), None)
            extra_part = (jnp.where(in_use, extra_part[0], lowest), jnp.where(in_use, extra_part[1], 0.0), jnp.where(in_use, extra_part[2], 0.0))
            running = combine_stats(running, extra_part)
        attended = running[2] / running[1][..., None]
        return jnp.transpose(attended, (2, 0, 1, 3)).reshape(BLOCK, QH * HD).astype(jnp.bfloat16)
    blocks_out = lax.map(one_block, jnp.arange(NB, dtype=jnp.int32))
    return blocks_out.reshape(NB * BLOCK, QH * HD)
```

```python
import math

import jax
import jax.numpy as jnp
from jax import lax
from jax.experimental import pallas as pl
from jax.experimental.pallas import tpu as pltpu
from jax.sharding import PartitionSpec as P

HD = 128
BLOCK = 512
SHARE = 4
ROWS = BLOCK // SHARE
LOWEST = -1e30
SCALE = 1.0 / math.sqrt(HD)
LOG2E = math.log2(math.e)


def frequency_table(columns):
    inverse = 1.0 / 500000.0 ** (jnp.arange(0, columns, 2, dtype=jnp.float32) / columns)
    wavelength = 2.0 * math.pi / inverse
    smooth = (8192.0 / wavelength - 1.0) / 3.0
    blended = (1.0 - smooth) * inverse / 8.0 + smooth * inverse
    return jnp.where(
        wavelength < 2048.0, inverse, jnp.where(wavelength > 8192.0, inverse / 8.0, blended)
    )


def rope_kernel(heads, cos_ref, sin_ref, x_ref, o_ref):
    cosine = cos_ref[...]
    sine = sin_ref[...]
    for h in range(heads):
        x = x_ref[:, h * HD : (h + 1) * HD].astype(jnp.float32)
        turned = x * cosine + pltpu.roll(x, HD // 2, 1) * sine
        o_ref[:, h * HD : (h + 1) * HD] = turned.astype(jnp.bfloat16)


def kv_kernel(heads, cos_ref, sin_ref, k_ref, v_ref, o_ref):
    cosine = cos_ref[...]
    sine = sin_ref[...]
    for h in range(heads):
        x = k_ref[:, h * HD : (h + 1) * HD].astype(jnp.float32)
        turned = x * cosine + pltpu.roll(x, HD // 2, 1) * sine
        o_ref[h, :, :HD] = turned.astype(jnp.bfloat16)
        o_ref[h, :, HD:] = v_ref[:, h * HD : (h + 1) * HD]


def stacked_queries(q_ref):
    return jnp.concatenate([q_ref[:, h * HD : (h + 1) * HD] for h in range(SHARE)], axis=0)


def attend(q, kv, mask, m, l, acc):
    s = lax.dot_general(
        q, kv[:, :HD], (((1,), (1,)), ((), ())), preferred_element_type=jnp.float32
    ) * (SCALE * LOG2E)
    if mask is not None:
        s = jnp.where(mask, s, LOWEST)
    top = jnp.max(s, axis=1, keepdims=True)
    if m is not None:
        top = jnp.maximum(m, top)
    p = jnp.exp2(s - top)
    total = jnp.sum(p, axis=1, keepdims=True)
    product = jnp.dot(p.astype(jnp.bfloat16), kv[:, HD:], preferred_element_type=jnp.float32)
    if m is not None:
        keep = jnp.exp2(m - top)
        total = total + l * keep
        product = product + acc * keep
    return top, total, product


def near_kernel(table_ref, rank_ref, q_ref, own_ref, acc_ref, m_ref, l_ref):
    b = pl.program_id(0)
    q = stacked_queries(q_ref)
    row = lax.broadcasted_iota(jnp.int32, (SHARE * ROWS, BLOCK), 0) % ROWS + rank_ref[0] * ROWS
    col = lax.broadcasted_iota(jnp.int32, (SHARE * ROWS, BLOCK), 1)
    m, l, acc = attend(q, own_ref[:, b].reshape(BLOCK, 2 * HD), row >= col, None, None, None)
    m_ref[0] = m
    l_ref[0] = l
    acc_ref[0] = acc
    for slot in range(3):
        target = table_ref[b * 3 + slot]

        @pl.when(target >= 0)
        def _():
            kv = own_ref[:, jnp.maximum(target, 0)].reshape(BLOCK, 2 * HD)
            m, l, acc = attend(q, kv, None, m_ref[0], l_ref[0], acc_ref[0])
            m_ref[0] = m
            l_ref[0] = l
            acc_ref[0] = acc


def far_kernel(
    table_ref, q_ref, kv0_ref, kv1_ref, kv2_ref, acc_in, m_in, l_in, o_ref, acc_ref, m_ref, l_ref
):
    b = pl.program_id(0)
    q = stacked_queries(q_ref)
    m_ref[...] = m_in[0]
    l_ref[...] = l_in[0]
    acc_ref[...] = acc_in[0]
    for slot, kv_ref in enumerate((kv0_ref, kv1_ref, kv2_ref)):

        @pl.when(table_ref[b * 3 + slot] >= 0)
        def _():
            kv = kv_ref[0].reshape(BLOCK, 2 * HD)
            m, l, acc = attend(q, kv, None, m_ref[...], l_ref[...], acc_ref[...])
            m_ref[...] = m
            l_ref[...] = l
            acc_ref[...] = acc

    out = (acc_ref[...] / l_ref[...]).astype(jnp.bfloat16)
    for h in range(SHARE):
        o_ref[:, h * HD : (h + 1) * HD] = out[h * ROWS : (h + 1) * ROWS]


def local(queries, key_states, value_states, key_picks, positions):
    local_rows = queries.shape[0]
    kv_heads = key_states.shape[1] // HD
    query_heads = queries.shape[1] // HD
    head_devices = lax.axis_size("head")
    across = [[SHARE * g + r for g in range(kv_heads)] for r in range(SHARE)]
    within = [[SHARE * g + r for r in range(SHARE)] for g in range(kv_heads)]
    rank = lax.axis_index("head") % SHARE

    angles = positions.astype(jnp.float32)[:, None] * frequency_table(HD)[None, :]
    cosine = jnp.cos(angles)
    sine = jnp.sin(angles)
    cosine = jnp.concatenate([cosine, cosine], axis=1)
    sine = jnp.concatenate([-sine, sine], axis=1)

    sent_kv = pl.pallas_call(
        lambda *refs: kv_kernel(kv_heads, *refs),
        out_shape=jax.ShapeDtypeStruct((kv_heads, local_rows, 2 * HD), jnp.bfloat16),
        name="rope_kv",
    )(cosine, sine, key_states, value_states)
    part_kv = lax.all_to_all(
        sent_kv, "head", split_axis=0, concat_axis=0, axis_index_groups=across, tiled=True
    )
    blocks = part_kv.shape[0]
    own_kv = lax.all_gather(part_kv, "head", axis=0, axis_index_groups=within)

    first_block = lax.axis_index("seq") * blocks
    all_blocks = key_picks.shape[0]
    picks = key_picks.shape[1]
    public = min(picks, blocks)
    block_ids = jnp.arange(all_blocks, dtype=jnp.int32)
    block_group = block_ids // blocks
    picked_later = (key_picks[:, :, None] == block_ids[None, None, :]) & (
        block_group[:, None, None] > block_group[None, None, :]
    )
    is_public = jnp.any(picked_later, axis=(0, 1))
    slot_rank = (
        jnp.cumsum(is_public.reshape(-1, blocks).astype(jnp.int32), axis=1) - 1
    ).reshape(-1)
    place = block_group * public + slot_rank
    own_public = lax.dynamic_slice_in_dim(is_public, first_block, blocks, 0)
    own_rank = lax.dynamic_slice_in_dim(slot_rank, first_block, blocks, 0)
    slot_ids = jnp.arange(public, dtype=jnp.int32)
    chosen = jnp.sum(
        jnp.where(
            own_public[None, :] & (own_rank[None, :] == slot_ids[:, None]),
            jnp.arange(blocks, dtype=jnp.int32)[None, :],
            0,
        ),
        axis=1,
    )
    outgoing = jnp.concatenate(
        [lax.dynamic_slice_in_dim(own_kv, chosen[p], 1, 1) for p in range(public)], axis=1
    )
    outgoing = jnp.transpose(outgoing, (1, 0, 2, 3))
    held_kv = lax.all_gather(outgoing, "seq", axis=0, tiled=True)

    own_picks = lax.dynamic_slice_in_dim(key_picks, first_block, blocks, 0)
    row_block = first_block + jnp.arange(blocks, dtype=jnp.int32)[:, None]
    near = (own_picks >= first_block) & (own_picks < row_block)
    near_table = jnp.where(near, own_picks - first_block, -1).reshape(-1)
    far = own_picks < first_block
    pick_place = jnp.sum(
        jnp.where(own_picks[:, :, None] == block_ids[None, None, :], place[None, None, :], 0),
        axis=2,
    )
    far_table = jnp.where(far, pick_place, -1).reshape(-1)

    turned_queries = pl.pallas_call(
        lambda *refs: rope_kernel(query_heads, *refs),
        out_shape=jax.ShapeDtypeStruct(queries.shape, jnp.bfloat16),
        name="rope_q",
    )(cosine, sine, queries)
    group_queries = lax.all_to_all(
        turned_queries, "head", split_axis=1, concat_axis=0, axis_index_groups=across, tiled=True
    )
    tall = SHARE * ROWS
    wide = SHARE * HD
    stat = jax.ShapeDtypeStruct((blocks, tall, 1), jnp.float32)
    acc, m, l = pl.pallas_call(
        near_kernel,
        out_shape=(jax.ShapeDtypeStruct((blocks, tall, HD), jnp.float32), stat, stat),
        grid_spec=pltpu.PrefetchScalarGridSpec(
            num_scalar_prefetch=2,
            grid=(blocks,),
            in_specs=[
                pl.BlockSpec((ROWS, wide), lambda b, t, r: (b, 0)),
                pl.BlockSpec(own_kv.shape, lambda b, t, r: (0, 0, 0, 0)),
            ],
            out_specs=(
                pl.BlockSpec((1, tall, HD), lambda b, t, r: (b, 0, 0)),
                pl.BlockSpec((1, tall, 1), lambda b, t, r: (b, 0, 0)),
                pl.BlockSpec((1, tall, 1), lambda b, t, r: (b, 0, 0)),
            ),
        ),
        name="near_attention",
    )(near_table, rank.reshape(1), group_queries, own_kv)

    def held_spec(slot):
        return pl.BlockSpec(
            (1, SHARE, ROWS, 2 * HD), lambda b, t: (jnp.maximum(t[b * 3 + slot], 0), 0, 0, 0)
        )

    attended = pl.pallas_call(
        far_kernel,
        out_shape=jax.ShapeDtypeStruct(group_queries.shape, jnp.bfloat16),
        grid_spec=pltpu.PrefetchScalarGridSpec(
            num_scalar_prefetch=1,
            grid=(blocks,),
            in_specs=[
                pl.BlockSpec((ROWS, wide), lambda b, t: (b, 0)),
                held_spec(0),
                held_spec(1),
                held_spec(2),
                pl.BlockSpec((1, tall, HD), lambda b, t: (b, 0, 0)),
                pl.BlockSpec((1, tall, 1), lambda b, t: (b, 0, 0)),
                pl.BlockSpec((1, tall, 1), lambda b, t: (b, 0, 0)),
            ],
            out_specs=pl.BlockSpec((ROWS, wide), lambda b, t: (b, 0)),
            scratch_shapes=[
                pltpu.VMEM((tall, HD), jnp.float32),
                pltpu.VMEM((tall, 1), jnp.float32),
                pltpu.VMEM((tall, 1), jnp.float32),
            ],
        ),
        name="far_attention",
    )(far_table, group_queries, held_kv, held_kv, held_kv, acc, m, l)
    return lax.all_to_all(
        attended, "head", split_axis=0, concat_axis=1, axis_index_groups=across, tiled=True
    )


def solution(mesh):
    in_specs = (
        P(("seq", "head"), None),
        P(("seq", "head"), None),
        P(("seq", "head"), None),
        P(),
        P(("seq", "head")),
    )
    out_specs = P(("seq", "head"), None)
    return jax.shard_map(local, mesh=mesh, in_specs=in_specs, out_specs=out_specs, check_vma=False)
```

```python
import functools
import math

import jax
import jax.numpy as jnp
from jax import lax
from jax.experimental import pallas as pl
from jax.experimental.pallas import tpu as pltpu
from jax.sharding import PartitionSpec as P

HD = 128
BLOCK = 512
SHARE = 4
ROWS = BLOCK // SHARE
LOWEST = -1e30
SCALE = 1.0 / math.sqrt(HD)
MESH = pl.DeviceIdType.MESH
LOG2E = math.log2(math.e)


def frequency_table(columns):
    inverse = 1.0 / 500000.0 ** (jnp.arange(0, columns, 2, dtype=jnp.float32) / columns)
    wavelength = 2.0 * math.pi / inverse
    smooth = (8192.0 / wavelength - 1.0) / 3.0
    blended = (1.0 - smooth) * inverse / 8.0 + smooth * inverse
    return jnp.where(
        wavelength < 2048.0, inverse, jnp.where(wavelength > 8192.0, inverse / 8.0, blended)
    )


def rope_kernel(heads, cos_ref, sin_ref, x_ref, o_ref):
    cosine = cos_ref[...]
    sine = sin_ref[...]
    for h in range(heads):
        x = x_ref[:, h * HD : (h + 1) * HD].astype(jnp.float32)
        turned = x * cosine + pltpu.roll(x, HD // 2, 1) * sine
        o_ref[:, h * HD : (h + 1) * HD] = turned.astype(jnp.bfloat16)


def kv_kernel(heads, cos_ref, sin_ref, k_ref, v_ref, o_ref):
    cosine = cos_ref[...]
    sine = sin_ref[...]
    for h in range(heads):
        x = k_ref[:, h * HD : (h + 1) * HD].astype(jnp.float32)
        turned = x * cosine + pltpu.roll(x, HD // 2, 1) * sine
        o_ref[h, :, :HD] = turned.astype(jnp.bfloat16)
        o_ref[h, :, HD:] = v_ref[:, h * HD : (h + 1) * HD]


def attend(q, kv, mask, bias, carry):
    s = lax.dot_general(
        q, kv[:, :HD], (((1,), (1,)), ((), ())), preferred_element_type=jnp.float32
    ) * (SCALE * LOG2E)
    if mask is not None:
        s = jnp.where(mask, s, LOWEST)
    if bias is not None:
        s = s + bias
    top = jnp.max(s, axis=1, keepdims=True)
    if carry is not None:
        top = jnp.maximum(carry[0], top)
    p = jnp.exp2(s - top)
    total = jnp.sum(p, axis=1, keepdims=True)
    product = jnp.dot(p.astype(jnp.bfloat16), kv[:, HD:], preferred_element_type=jnp.float32)
    if carry is not None:
        keep = jnp.exp2(carry[0] - top)
        total = total + carry[1] * keep
        product = product + carry[2] * keep
    return top, total, product


def group_kernel(
    blocks,
    public,
    ring,
    chosen_ref,
    place_ref,
    bias_ref,
    kv_in,
    q_in,
    o_ref,
    own_kv,
    kv_all,
    q_all,
    out_buf,
    send_sem,
    kv_sem,
    fy_sem,
    fz_sem,
    q_sem,
    ag_sem,
    o_sem,
    local_sem,
):
    s = lax.axis_index("seq")
    d = lax.axis_index("head")
    g, r = d // SHARE, d % SHARE
    x, y_lo, core = s // 4, (s // 2) % 2, s % 2
    z_par, y_hi = r // 2, r % 2
    wide = SHARE * HD
    heads = blocks

    def at_x(step):
        return ((x + step + ring) % ring) * 4 + s % 4

    def across(step):
        return (s, ((g + step + heads) % heads) * SHARE + r)

    y_flip = d + 1 - 2 * y_hi
    y_peer = (s, y_flip)
    z_peer = (s, d + 2 - 4 * z_par)
    s_flip = s + 2 - 4 * y_lo
    y_near, y_far = (s_flip, d), (s_flip, y_flip)
    core_peer = (s + 1 - 2 * core, d)
    x_next, x_last = (at_x(1), d), (at_x(-1), d)
    partners = [across(j) for j in range(1, heads)]
    partners += [y_peer, z_peer, y_near, y_far, core_peer, x_next, x_last]

    barrier = pltpu.get_barrier_semaphore()
    for peer in partners:
        pl.semaphore_signal(barrier, inc=1, device_id=peer, device_id_type=MESH)
    pl.semaphore_wait(barrier, len(partners))

    pending = []

    def send(source, target, arrival, peer):
        copy = pltpu.make_async_remote_copy(
            src_ref=source,
            dst_ref=target,
            send_sem=send_sem.at[len(pending)],
            recv_sem=arrival,
            device_id=peer,
            device_id_type=MESH,
        )
        copy.start()
        pending.append(copy)

    def arrived(region, arrival):
        pltpu.make_async_remote_copy(
            src_ref=region,
            dst_ref=region,
            send_sem=send_sem.at[0],
            recv_sem=arrival,
            device_id=core_peer,
            device_id_type=MESH,
        ).wait_recv()

    def away(step):
        return (g + step + heads) % heads

    order = []
    for j in range(1, heads // 2 + 1):
        order += [j] if 2 * j == heads else [j, heads - j]

    own_local = pltpu.make_async_copy(kv_in.at[g], own_kv.at[g, r], local_sem.at[0])
    own_local.start()
    for j in order:
        send(kv_in.at[away(j)], own_kv.at[g, r], kv_sem.at[j], across(j))
    query_local = pltpu.make_async_copy(
        q_in.at[:, pl.ds(pl.multiple_of(g * wide, wide), wide)], q_all.at[g], local_sem.at[1]
    )
    query_local.start()
    r_y, r_z = r + 1 - 2 * y_hi, r + 2 - 4 * z_par
    r_zy = r_y + 2 - 4 * z_par
    for j in [0] + order:
        region = own_kv.at[away(-j), r]
        if j == 0:
            own_local.wait()
        else:
            arrived(region, kv_sem.at[j])
        send(region, region, fy_sem.at[j], y_peer)
        send(region, region, fz_sem.at[0, j], z_peer)
    for j in [0] + order:
        region = own_kv.at[away(-j), r_y]
        arrived(region, fy_sem.at[j])
        send(region, region, fz_sem.at[1, j], z_peer)
    for j in order:
        send(
            q_in.at[:, pl.ds(pl.multiple_of(away(j) * wide, wide), wide)],
            q_all.at[g],
            q_sem.at[j],
            across(j),
        )
    for j in [0] + order:
        arrived(own_kv.at[away(-j), r_z], fz_sem.at[0, j])
        arrived(own_kv.at[away(-j), r_zy], fz_sem.at[1, j])

    for p in range(public):
        kv_all[blocks + public * s + p] = own_kv[chosen_ref[p]]
    own_copy = pltpu.make_async_copy(own_kv, kv_all.at[pl.ds(0, blocks)], local_sem.at[2])
    own_copy.start()

    def unit(where, half=None):
        rows = pl.ds(blocks + public * where, public)
        if half is None:
            return kv_all.at[rows]
        return kv_all.at[rows, pl.ds(half * (SHARE // 2), SHARE // 2)]

    steps = (0, -1, 1, 2)
    whole = unit(s)
    send(whole, whole, ag_sem.at[0], x_next)
    send(whole, whole, ag_sem.at[1], x_last)
    for half, peer in ((0, y_near), (1, y_far)):
        region = unit(s, half)
        send(region, region, ag_sem.at[4 + half], peer)
    send(whole, whole, ag_sem.at[12], core_peer)
    for k, half, peer in ((1, 0, x_next), (2, 1, x_last)):
        where = at_x(steps[k])
        arrived(unit(where), ag_sem.at[k - 1])
        region = unit(where, half)
        send(region, region, ag_sem.at[2 + half], peer)
        for part, side in ((0, y_near), (1, y_far)):
            region = unit(where, part)
            send(region, region, ag_sem.at[4 + 2 * k + part], side)
        send(unit(where), unit(where), ag_sem.at[12 + k], core_peer)
    for half, peer in ((0, y_near), (1, y_far)):
        region = unit(at_x(2), half)
        arrived(region, ag_sem.at[2 + half])
        send(region, region, ag_sem.at[10 + half], peer)
        send(region, region, ag_sem.at[15 + half], core_peer)
    for k in range(4):
        where = at_x(steps[k]) + 2 - 4 * y_lo
        for half in range(2):
            region = unit(where, half)
            arrived(region, ag_sem.at[4 + 2 * k + half])
            send(region, region, ag_sem.at[17 + 2 * k + half], core_peer)
    other = 1 - 2 * core
    for k in range(3):
        arrived(unit(at_x(steps[k]) + other), ag_sem.at[12 + k])
    for half in range(2):
        arrived(unit(at_x(2) + other, half), ag_sem.at[15 + half])
    for k in range(4):
        where = at_x(steps[k]) + 2 - 4 * y_lo + other
        for half in range(2):
            arrived(unit(where, half), ag_sem.at[17 + 2 * k + half])
    own_copy.wait()
    query_local.wait()
    for j in order:
        arrived(q_all.at[away(-j)], q_sem.at[j])

    tall = SHARE * ROWS
    row = lax.broadcasted_iota(jnp.int32, (tall, BLOCK), 0) % ROWS + r * ROWS
    col = lax.broadcasted_iota(jnp.int32, (tall, BLOCK), 1)
    causal = row >= col
    mine = pl.ds(pl.multiple_of(g * wide, wide), wide)
    base = len(pending)

    def home(j):
        return pltpu.make_async_remote_copy(
            src_ref=out_buf.at[j],
            dst_ref=o_ref.at[:, mine],
            send_sem=send_sem.at[base + j],
            recv_sem=o_sem.at[j],
            device_id=(s, ((g + 1 + j) % heads) * SHARE + r),
            device_id_type=MESH,
        )

    def one_block(j, _):
        b = (g + 1 + j) % heads
        q = jnp.concatenate([q_all[b, :, h * HD : (h + 1) * HD] for h in range(SHARE)], axis=0)
        carry = attend(q, kv_all[b].reshape(BLOCK, 2 * HD), causal, None, None)

        @pl.when(j > 0)
        def _():
            home(j - 1).start()

        for slot in range(3):
            kv = kv_all[place_ref[b * 3 + slot]].reshape(BLOCK, 2 * HD)
            carry = attend(q, kv, None, bias_ref[b * 3 + slot], carry)
        out = (carry[2] / carry[1]).astype(jnp.bfloat16)
        for h in range(SHARE):
            out_buf[j, :, h * HD : (h + 1) * HD] = out[h * ROWS : (h + 1) * ROWS]
        return 0

    lax.fori_loop(0, heads, one_block, 0)
    last = pltpu.make_async_copy(out_buf.at[heads - 1], o_ref.at[:, mine], local_sem.at[3])
    last.start()
    for copy in pending:
        copy.wait_send()
    for j in range(heads - 1):
        columns = pl.ds(pl.multiple_of(away(-1 - j) * wide, wide), wide)
        arrived(o_ref.at[:, columns], o_sem.at[j])
        home(j).wait_send()
    last.wait()


def local(queries, key_states, value_states, key_picks, positions):
    local_rows = queries.shape[0]
    kv_heads = key_states.shape[1] // HD
    query_heads = queries.shape[1] // HD

    angles = positions.astype(jnp.float32)[:, None] * frequency_table(HD)[None, :]
    cosine = jnp.cos(angles)
    sine = jnp.sin(angles)
    cosine = jnp.concatenate([cosine, cosine], axis=1)
    sine = jnp.concatenate([-sine, sine], axis=1)

    sent_kv = pl.pallas_call(
        lambda *refs: kv_kernel(kv_heads, *refs),
        out_shape=jax.ShapeDtypeStruct((kv_heads, local_rows, 2 * HD), jnp.bfloat16),
        name="rope_kv",
    )(cosine, sine, key_states, value_states)
    turned_queries = pl.pallas_call(
        lambda *refs: rope_kernel(query_heads, *refs),
        out_shape=jax.ShapeDtypeStruct(queries.shape, jnp.bfloat16),
        name="rope_q",
    )(cosine, sine, queries)

    groups = lax.axis_size("seq")
    all_blocks, picks = key_picks.shape
    blocks = all_blocks // groups
    first_block = lax.axis_index("seq") * blocks
    public = min(picks, blocks)
    block_ids = jnp.arange(all_blocks, dtype=jnp.int32)
    block_group = block_ids // blocks
    picked_later = (key_picks[:, :, None] == block_ids[None, None, :]) & (
        block_group[:, None, None] > block_group[None, None, :]
    )
    is_public = jnp.any(picked_later, axis=(0, 1))
    slot_rank = (
        jnp.cumsum(is_public.reshape(-1, blocks).astype(jnp.int32), axis=1) - 1
    ).reshape(-1)
    place = block_group * public + slot_rank
    own_public = lax.dynamic_slice_in_dim(is_public, first_block, blocks, 0)
    own_rank = lax.dynamic_slice_in_dim(slot_rank, first_block, blocks, 0)
    slot_ids = jnp.arange(public, dtype=jnp.int32)
    chosen = jnp.sum(
        jnp.where(
            own_public[None, :] & (own_rank[None, :] == slot_ids[:, None]),
            jnp.arange(blocks, dtype=jnp.int32)[None, :],
            0,
        ),
        axis=1,
    )
    own_picks = lax.dynamic_slice_in_dim(key_picks, first_block, blocks, 0)
    row_block = first_block + jnp.arange(blocks, dtype=jnp.int32)[:, None]
    near = (own_picks >= first_block) & (own_picks < row_block)
    far = own_picks < first_block
    pick_place = jnp.sum(
        jnp.where(own_picks[:, :, None] == block_ids[None, None, :], place[None, None, :], 0),
        axis=2,
    )
    held = jnp.where(near, own_picks - first_block, jnp.where(far, blocks + pick_place, 0))
    bias = jnp.where(near | far, 0.0, LOWEST).astype(jnp.float32)

    smem = pl.BlockSpec(memory_space=pltpu.SMEM)
    anywhere = pl.BlockSpec(memory_space=pl.ANY)
    copies = 2 * (kv_heads - 1) + 3 * kv_heads + 25 + (kv_heads - 1)
    return pl.pallas_call(
        functools.partial(group_kernel, blocks, public, groups // 4),
        out_shape=jax.ShapeDtypeStruct(queries.shape, jnp.bfloat16),
        in_specs=[smem, smem, smem, anywhere, anywhere],
        out_specs=anywhere,
        scratch_shapes=[
            pltpu.VMEM((blocks, SHARE, ROWS, 2 * HD), jnp.bfloat16),
            pltpu.VMEM((blocks + groups * public, SHARE, ROWS, 2 * HD), jnp.bfloat16),
            pltpu.VMEM((blocks, ROWS, SHARE * HD), jnp.bfloat16),
            pltpu.VMEM((blocks, ROWS, SHARE * HD), jnp.bfloat16),
            pltpu.SemaphoreType.DMA((copies,)),
            pltpu.SemaphoreType.DMA((kv_heads,)),
            pltpu.SemaphoreType.DMA((kv_heads,)),
            pltpu.SemaphoreType.DMA((2, kv_heads)),
            pltpu.SemaphoreType.DMA((kv_heads,)),
            pltpu.SemaphoreType.DMA((25,)),
            pltpu.SemaphoreType.DMA((kv_heads,)),
            pltpu.SemaphoreType.DMA((4,)),
        ],
        compiler_params=pltpu.CompilerParams(
            collective_id=0, has_side_effects=True, vmem_limit_bytes=48 << 20
        ),
        name="group_attention",
    )(chosen, held.reshape(-1), bias.reshape(-1), sent_kv, turned_queries)


def solution(mesh):
    in_specs = (
        P(("seq", "head"), None),
        P(("seq", "head"), None),
        P(("seq", "head"), None),
        P(),
        P(("seq", "head")),
    )
    out_specs = P(("seq", "head"), None)
    return jax.shard_map(local, mesh=mesh, in_specs=in_specs, out_specs=out_specs, check_vma=False)
```

```python
import functools
import math

import jax
import jax.numpy as jnp
from jax import lax
from jax.experimental import pallas as pl
from jax.experimental.pallas import tpu as pltpu
from jax.sharding import PartitionSpec as P

HD = 128
BLOCK = 512
SHARE = 4
ROWS = BLOCK // SHARE
LOWEST = -1e30
SCALE = 1.0 / math.sqrt(HD)
MESH = pl.DeviceIdType.MESH
LOG2E = math.log2(math.e)


def frequency_table(columns):
    inverse = 1.0 / 500000.0 ** (jnp.arange(0, columns, 2, dtype=jnp.float32) / columns)
    wavelength = 2.0 * math.pi / inverse
    smooth = (8192.0 / wavelength - 1.0) / 3.0
    blended = (1.0 - smooth) * inverse / 8.0 + smooth * inverse
    return jnp.where(
        wavelength < 2048.0, inverse, jnp.where(wavelength > 8192.0, inverse / 8.0, blended)
    )


def rope_kernel(heads, cos_ref, sin_ref, x_ref, o_ref):
    cosine = cos_ref[...]
    sine = sin_ref[...]
    for h in range(heads):
        x = x_ref[:, h * HD : (h + 1) * HD].astype(jnp.float32)
        turned = x * cosine + pltpu.roll(x, HD // 2, 1) * sine
        o_ref[:, h * HD : (h + 1) * HD] = turned.astype(jnp.bfloat16)


def kv_kernel(heads, cos_ref, sin_ref, k_ref, v_ref, o_ref):
    cosine = cos_ref[...]
    sine = sin_ref[...]
    for h in range(heads):
        x = k_ref[:, h * HD : (h + 1) * HD].astype(jnp.float32)
        turned = x * cosine + pltpu.roll(x, HD // 2, 1) * sine
        o_ref[h, :, :HD] = turned.astype(jnp.bfloat16)
        o_ref[h, :, HD:] = v_ref[:, h * HD : (h + 1) * HD]


def attend(q, kv, mask, bias, carry):
    s = lax.dot_general(
        q, kv[:, :HD], (((1,), (1,)), ((), ())), preferred_element_type=jnp.float32
    ) * (SCALE * LOG2E)
    if mask is not None:
        s = jnp.where(mask, s, LOWEST)
    if bias is not None:
        s = s + bias
    top = jnp.max(s, axis=1, keepdims=True)
    if carry is not None:
        top = jnp.maximum(carry[0], top)
    p = jnp.exp2(s - top)
    total = jnp.sum(p, axis=1, keepdims=True)
    product = jnp.dot(p.astype(jnp.bfloat16), kv[:, HD:], preferred_element_type=jnp.float32)
    if carry is not None:
        keep = jnp.exp2(carry[0] - top)
        total = total + carry[1] * keep
        product = product + carry[2] * keep
    return top, total, product


def group_kernel(
    blocks,
    public,
    ring,
    chosen_ref,
    place_ref,
    bias_ref,
    kv_in,
    q_in,
    o_ref,
    own_a,
    own_b,
    kv_all,
    q_all,
    out_buf,
    send_sem,
    kv_sem,
    fy_sem,
    fz_sem,
    q_sem,
    ag_sem,
    o_sem,
    local_sem,
):
    s = lax.axis_index("seq")
    d = lax.axis_index("head")
    g, r = d // SHARE, d % SHARE
    x, y_lo, core = s // 4, (s // 2) % 2, s % 2
    z_par, y_hi = r // 2, r % 2
    wide = SHARE * HD
    heads = blocks

    def at_x(step):
        return ((x + step + ring) % ring) * 4 + s % 4

    def across(step):
        return (s, ((g + step + heads) % heads) * SHARE + r)

    y_flip = d + 1 - 2 * y_hi
    y_peer = (s, y_flip)
    z_peer = (s, d + 2 - 4 * z_par)
    s_flip = s + 2 - 4 * y_lo
    y_near, y_far = (s_flip, d), (s_flip, y_flip)
    core_peer = (s + 1 - 2 * core, d)
    x_next, x_last = (at_x(1), d), (at_x(-1), d)
    partners = [across(j) for j in range(1, heads)]
    partners += [y_peer, z_peer, y_near, y_far, core_peer, x_next, x_last]

    barrier = pltpu.get_barrier_semaphore()
    for peer in partners:
        pl.semaphore_signal(barrier, inc=1, device_id=peer, device_id_type=MESH)
    pl.semaphore_wait(barrier, len(partners))

    pending = []

    def send(source, target, arrival, peer):
        copy = pltpu.make_async_remote_copy(
            src_ref=source,
            dst_ref=target,
            send_sem=send_sem.at[len(pending)],
            recv_sem=arrival,
            device_id=peer,
            device_id_type=MESH,
        )
        copy.start()
        pending.append(copy)

    def arrived(region, arrival):
        pltpu.make_async_remote_copy(
            src_ref=region,
            dst_ref=region,
            send_sem=send_sem.at[0],
            recv_sem=arrival,
            device_id=core_peer,
            device_id_type=MESH,
        ).wait_recv()

    def away(step):
        return (g + step + heads) % heads

    order = []
    for j in range(1, heads // 2 + 1):
        order += [j] if 2 * j == heads else [j, heads - j]

    own_local = pltpu.make_async_copy(kv_in.at[g], own_a.at[g, y_hi], local_sem.at[0])
    own_local.start()
    for j in order:
        send(kv_in.at[away(j)], own_a.at[g, y_hi], kv_sem.at[j], across(j))
    query_local = pltpu.make_async_copy(
        q_in.at[:, pl.ds(pl.multiple_of(g * wide, wide), wide)], q_all.at[g], local_sem.at[1]
    )
    query_local.start()
    for j in [0] + order:
        region = own_a.at[away(-j), y_hi]
        if j == 0:
            own_local.wait()
        else:
            arrived(region, kv_sem.at[j])
        send(region, own_b.at[away(-j), y_hi], fz_sem.at[j], z_peer)
        send(region, region, fy_sem.at[0, j], y_peer)
    for j in [0] + order:
        region = own_b.at[away(-j), y_hi]
        arrived(region, fz_sem.at[j])
        send(region, region, fy_sem.at[1, j], y_peer)
    for j in order:
        send(
            q_in.at[:, pl.ds(pl.multiple_of(away(j) * wide, wide), wide)],
            q_all.at[g],
            q_sem.at[j],
            across(j),
        )

    half_rows = SHARE // 2
    halves = (z_par, 1 - z_par)
    steps = (0, -1, 1, 2)

    def unit(where, h):
        rows = pl.ds(blocks + public * where, public)
        return kv_all.at[rows, pl.ds(halves[h] * half_rows, half_rows)]

    def x_arrival(k, h):
        return ag_sem.at[2 * (k - 1) + h]

    def y_arrival(k, h):
        return ag_sem.at[6 + 2 * k + h]

    def core_arrival(column, k, h):
        return ag_sem.at[14 + 8 * column + 2 * k + h]

    sides = (y_near, y_far)
    own_copies = []
    for h, own in ((0, own_a), (1, own_b)):
        for j in [0] + order:
            arrived(own.at[away(-j), 1 - y_hi], fy_sem.at[h, j])
        part = pl.ds(halves[h] * half_rows, half_rows)
        for p in range(public):
            kv_all[blocks + public * s + p, part] = own[chosen_ref[p]]
        own_copies.append(
            pltpu.make_async_copy(own, kv_all.at[pl.ds(0, blocks), part], local_sem.at[2 + h])
        )
        own_copies[-1].start()
        region = unit(s, h)
        send(region, region, x_arrival(1, h), x_next)
        send(region, region, x_arrival(2, h), x_last)
        send(region, region, y_arrival(0, h), sides[h])
        send(region, region, core_arrival(0, 0, h), core_peer)
    for h in range(2):
        for k, onward in ((1, x_next), (2, x_last)):
            region = unit(at_x(steps[k]), h)
            arrived(region, x_arrival(k, h))
            if h == k - 1:
                send(region, region, x_arrival(3, h), onward)
            send(region, region, y_arrival(k, h), sides[h])
            send(region, region, core_arrival(0, k, h), core_peer)
    for h in range(2):
        region = unit(at_x(2), h)
        arrived(region, x_arrival(3, h))
        send(region, region, y_arrival(3, h), sides[h])
        send(region, region, core_arrival(0, 3, h), core_peer)
    for k in range(4):
        for h in range(2):
            region = unit(at_x(steps[k]) + 2 - 4 * y_lo, h)
            arrived(region, y_arrival(k, h))
            send(region, region, core_arrival(1, k, h), core_peer)
    for column in range(2):
        for k in range(4):
            where = at_x(steps[k]) + column * (2 - 4 * y_lo) + 1 - 2 * core
            for h in range(2):
                arrived(unit(where, h), core_arrival(column, k, h))
    for copy in own_copies:
        copy.wait()
    query_local.wait()
    for j in order:
        arrived(q_all.at[away(-j)], q_sem.at[j])

    tall = SHARE * ROWS
    row = lax.broadcasted_iota(jnp.int32, (tall, BLOCK), 0) % ROWS + r * ROWS
    col = lax.broadcasted_iota(jnp.int32, (tall, BLOCK), 1)
    causal = row >= col
    mine = pl.ds(pl.multiple_of(g * wide, wide), wide)
    base = len(pending)

    def offset(j):
        return (1 - 2 * (j % 2)) * (heads // 2 - (j + 1) // 2)

    def home(j):
        return pltpu.make_async_remote_copy(
            src_ref=out_buf.at[j],
            dst_ref=o_ref.at[:, mine],
            send_sem=send_sem.at[base + j],
            recv_sem=o_sem.at[j],
            device_id=across(offset(j)),
            device_id_type=MESH,
        )

    def one_block(j, _):
        b = away(offset(j))
        q = jnp.concatenate([q_all[b, :, h * HD : (h + 1) * HD] for h in range(SHARE)], axis=0)
        carry = attend(q, kv_all[b].reshape(BLOCK, 2 * HD), causal, None, None)

        @pl.when(j > 0)
        def _():
            home(j - 1).start()

        for slot in range(3):
            kv = kv_all[place_ref[b * 3 + slot]].reshape(BLOCK, 2 * HD)
            carry = attend(q, kv, None, bias_ref[b * 3 + slot], carry)
        out = (carry[2] / carry[1]).astype(jnp.bfloat16)
        for h in range(SHARE):
            out_buf[j, :, h * HD : (h + 1) * HD] = out[h * ROWS : (h + 1) * ROWS]
        return 0

    lax.fori_loop(0, heads, one_block, 0)
    last = pltpu.make_async_copy(out_buf.at[heads - 1], o_ref.at[:, mine], local_sem.at[4])
    last.start()
    for copy in pending:
        copy.wait_send()
    for j in range(heads - 1):
        columns = pl.ds(pl.multiple_of(away(-offset(j)) * wide, wide), wide)
        arrived(o_ref.at[:, columns], o_sem.at[j])
        home(j).wait_send()
    last.wait()


def local(queries, key_states, value_states, key_picks, positions):
    local_rows = queries.shape[0]
    kv_heads = key_states.shape[1] // HD
    query_heads = queries.shape[1] // HD

    angles = positions.astype(jnp.float32)[:, None] * frequency_table(HD)[None, :]
    cosine = jnp.cos(angles)
    sine = jnp.sin(angles)
    cosine = jnp.concatenate([cosine, cosine], axis=1)
    sine = jnp.concatenate([-sine, sine], axis=1)

    sent_kv = pl.pallas_call(
        lambda *refs: kv_kernel(kv_heads, *refs),
        out_shape=jax.ShapeDtypeStruct((kv_heads, local_rows, 2 * HD), jnp.bfloat16),
        name="rope_kv",
    )(cosine, sine, key_states, value_states)
    turned_queries = pl.pallas_call(
        lambda *refs: rope_kernel(query_heads, *refs),
        out_shape=jax.ShapeDtypeStruct(queries.shape, jnp.bfloat16),
        name="rope_q",
    )(cosine, sine, queries)

    groups = lax.axis_size("seq")
    all_blocks, picks = key_picks.shape
    blocks = all_blocks // groups
    first_block = lax.axis_index("seq") * blocks
    public = min(picks, blocks)
    block_ids = jnp.arange(all_blocks, dtype=jnp.int32)
    block_group = block_ids // blocks
    picked_later = (key_picks[:, :, None] == block_ids[None, None, :]) & (
        block_group[:, None, None] > block_group[None, None, :]
    )
    is_public = jnp.any(picked_later, axis=(0, 1))
    slot_rank = (
        jnp.cumsum(is_public.reshape(-1, blocks).astype(jnp.int32), axis=1) - 1
    ).reshape(-1)
    place = block_group * public + slot_rank
    own_public = lax.dynamic_slice_in_dim(is_public, first_block, blocks, 0)
    own_rank = lax.dynamic_slice_in_dim(slot_rank, first_block, blocks, 0)
    slot_ids = jnp.arange(public, dtype=jnp.int32)
    chosen = jnp.sum(
        jnp.where(
            own_public[None, :] & (own_rank[None, :] == slot_ids[:, None]),
            jnp.arange(blocks, dtype=jnp.int32)[None, :],
            0,
        ),
        axis=1,
    )
    own_picks = lax.dynamic_slice_in_dim(key_picks, first_block, blocks, 0)
    row_block = first_block + jnp.arange(blocks, dtype=jnp.int32)[:, None]
    near = (own_picks >= first_block) & (own_picks < row_block)
    far = own_picks < first_block
    pick_place = jnp.sum(
        jnp.where(own_picks[:, :, None] == block_ids[None, None, :], place[None, None, :], 0),
        axis=2,
    )
    held = jnp.where(near, own_picks - first_block, jnp.where(far, blocks + pick_place, 0))
    bias = jnp.where(near | far, 0.0, LOWEST).astype(jnp.float32)

    smem = pl.BlockSpec(memory_space=pltpu.SMEM)
    vmem = pl.BlockSpec(memory_space=pltpu.VMEM)
    anywhere = pl.BlockSpec(memory_space=pl.ANY)
    copies = 2 * (kv_heads - 1) + 3 * kv_heads + 30 + (kv_heads - 1)
    return pl.pallas_call(
        functools.partial(group_kernel, blocks, public, groups // 4),
        out_shape=jax.ShapeDtypeStruct(queries.shape, jnp.bfloat16),
        in_specs=[smem, smem, smem, vmem, vmem],
        out_specs=anywhere,
        scratch_shapes=[
            pltpu.VMEM((blocks, SHARE // 2, ROWS, 2 * HD), jnp.bfloat16),
            pltpu.VMEM((blocks, SHARE // 2, ROWS, 2 * HD), jnp.bfloat16),
            pltpu.VMEM((blocks + groups * public, SHARE, ROWS, 2 * HD), jnp.bfloat16),
            pltpu.VMEM((blocks, ROWS, SHARE * HD), jnp.bfloat16),
            pltpu.VMEM((blocks, ROWS, SHARE * HD), jnp.bfloat16),
            pltpu.SemaphoreType.DMA((copies,)),
            pltpu.SemaphoreType.DMA((kv_heads,)),
            pltpu.SemaphoreType.DMA((2, kv_heads)),
            pltpu.SemaphoreType.DMA((kv_heads,)),
            pltpu.SemaphoreType.DMA((kv_heads,)),
            pltpu.SemaphoreType.DMA((30,)),
            pltpu.SemaphoreType.DMA((kv_heads,)),
            pltpu.SemaphoreType.DMA((5,)),
        ],
        compiler_params=pltpu.CompilerParams(
            collective_id=0, has_side_effects=True, vmem_limit_bytes=48 << 20
        ),
        name="group_attention",
    )(chosen, held.reshape(-1), bias.reshape(-1), sent_kv, turned_queries)


def solution(mesh):
    in_specs = (
        P(("seq", "head"), None),
        P(("seq", "head"), None),
        P(("seq", "head"), None),
        P(),
        P(("seq", "head")),
    )
    out_specs = P(("seq", "head"), None)
    return jax.shard_map(local, mesh=mesh, in_specs=in_specs, out_specs=out_specs, check_vma=False)
```

```python
import functools
import math

import jax
import jax.numpy as jnp
from jax import lax
from jax.experimental import pallas as pl
from jax.experimental.pallas import tpu as pltpu
from jax.sharding import PartitionSpec as P

HD = 128
BLOCK = 512
SHARE = 4
ROWS = BLOCK // SHARE
LOWEST = -1e30
SCALE = 1.0 / math.sqrt(HD)
MESH = pl.DeviceIdType.MESH
LOG2E = math.log2(math.e)


def frequency_table(columns):
    inverse = 1.0 / 500000.0 ** (jnp.arange(0, columns, 2, dtype=jnp.float32) / columns)
    wavelength = 2.0 * math.pi / inverse
    smooth = (8192.0 / wavelength - 1.0) / 3.0
    blended = (1.0 - smooth) * inverse / 8.0 + smooth * inverse
    return jnp.where(
        wavelength < 2048.0, inverse, jnp.where(wavelength > 8192.0, inverse / 8.0, blended)
    )


def turn(x, cosine, sine):
    x = x.astype(jnp.float32)
    return (x * cosine + pltpu.roll(x, HD // 2, 1) * sine).astype(jnp.bfloat16)


def attend(q, kv, mask, bias, carry):
    s = lax.dot_general(
        q, kv[:, :HD], (((1,), (1,)), ((), ())), preferred_element_type=jnp.float32
    ) * (SCALE * LOG2E)
    if mask is not None:
        s = jnp.where(mask, s, LOWEST)
    if bias is not None:
        s = s + bias
    top = jnp.max(s, axis=1, keepdims=True)
    if carry is not None:
        top = jnp.maximum(carry[0], top)
    p = jnp.exp2(s - top)
    total = jnp.sum(p, axis=1, keepdims=True)
    product = jnp.dot(p.astype(jnp.bfloat16), kv[:, HD:], preferred_element_type=jnp.float32)
    if carry is not None:
        keep = jnp.exp2(carry[0] - top)
        total = total + carry[1] * keep
        product = product + carry[2] * keep
    return top, total, product


def group_kernel(
    blocks,
    public,
    ring,
    chosen_ref,
    place_ref,
    bias_ref,
    cos_ref,
    sin_ref,
    k_ref,
    v_ref,
    q_ref,
    o_ref,
    kv_in,
    q_in,
    own_a,
    own_b,
    kv_all,
    q_all,
    out_buf,
    send_sem,
    kv_sem,
    fy_sem,
    fz_sem,
    q_sem,
    ag_sem,
    o_sem,
    local_sem,
):
    s = lax.axis_index("seq")
    d = lax.axis_index("head")
    g, r = d // SHARE, d % SHARE
    x, y_lo, core = s // 4, (s // 2) % 2, s % 2
    z_par, y_hi = r // 2, r % 2
    wide = SHARE * HD
    heads = blocks

    def at_x(step):
        return ((x + step + ring) % ring) * 4 + s % 4

    def across(step):
        return (s, ((g + step + heads) % heads) * SHARE + r)

    y_flip = d + 1 - 2 * y_hi
    y_peer = (s, y_flip)
    z_peer = (s, d + 2 - 4 * z_par)
    s_flip = s + 2 - 4 * y_lo
    y_near, y_far = (s_flip, d), (s_flip, y_flip)
    core_peer = (s + 1 - 2 * core, d)
    x_next, x_last = (at_x(1), d), (at_x(-1), d)
    partners = [across(j) for j in range(1, heads)]
    partners += [y_peer, z_peer, y_near, y_far, core_peer, x_next, x_last]

    barrier = pltpu.get_barrier_semaphore()
    for peer in partners:
        pl.semaphore_signal(barrier, inc=1, device_id=peer, device_id_type=MESH)
    raw = pltpu.make_async_copy(q_ref, q_in, local_sem.at[5])
    raw.start()
    for h in range(heads):
        lanes = slice(h * HD, (h + 1) * HD)
        kv_in[h, :, :HD] = turn(k_ref[:, lanes], cos_ref[...], sin_ref[...])
        kv_in[h, :, HD:] = v_ref[:, lanes]
    pl.semaphore_wait(barrier, len(partners))

    pending = []

    def send(source, target, arrival, peer):
        copy = pltpu.make_async_remote_copy(
            src_ref=source,
            dst_ref=target,
            send_sem=send_sem.at[len(pending)],
            recv_sem=arrival,
            device_id=peer,
            device_id_type=MESH,
        )
        copy.start()
        pending.append(copy)

    def arrived(region, arrival):
        pltpu.make_async_remote_copy(
            src_ref=region,
            dst_ref=region,
            send_sem=send_sem.at[0],
            recv_sem=arrival,
            device_id=core_peer,
            device_id_type=MESH,
        ).wait_recv()

    def away(step):
        return (g + step + heads) % heads

    order = []
    for j in range(1, heads // 2 + 1):
        order += [j] if 2 * j == heads else [j, heads - j]

    own_local = pltpu.make_async_copy(kv_in.at[g], own_a.at[g, y_hi], local_sem.at[0])
    own_local.start()
    for j in order:
        send(kv_in.at[away(j)], own_a.at[g, y_hi], kv_sem.at[j], across(j))
    raw.wait()
    for h in range(heads * SHARE):
        lanes = slice(h * HD, (h + 1) * HD)
        q_in[:, lanes] = turn(q_in[:, lanes], cos_ref[...], sin_ref[...])
    query_local = pltpu.make_async_copy(
        q_in.at[:, pl.ds(pl.multiple_of(g * wide, wide), wide)], q_all.at[g], local_sem.at[1]
    )
    query_local.start()
    for j in [0] + order:
        region = own_a.at[away(-j), y_hi]
        if j == 0:
            own_local.wait()
        else:
            arrived(region, kv_sem.at[j])
        send(region, own_b.at[away(-j), y_hi], fz_sem.at[j], z_peer)
        send(region, region, fy_sem.at[0, j], y_peer)
    for j in [0] + order:
        region = own_b.at[away(-j), y_hi]
        arrived(region, fz_sem.at[j])
        send(region, region, fy_sem.at[1, j], y_peer)
    for j in order:
        send(
            q_in.at[:, pl.ds(pl.multiple_of(away(j) * wide, wide), wide)],
            q_all.at[g],
            q_sem.at[j],
            across(j),
        )

    half_rows = SHARE // 2
    halves = (z_par, 1 - z_par)
    steps = (0, -1, 1, 2)

    def unit(where, h):
        rows = pl.ds(blocks + public * where, public)
        return kv_all.at[rows, pl.ds(halves[h] * half_rows, half_rows)]

    def x_arrival(k, h):
        return ag_sem.at[2 * (k - 1) + h]

    def y_arrival(k, h):
        return ag_sem.at[6 + 2 * k + h]

    def core_arrival(column, k, h):
        return ag_sem.at[14 + 8 * column + 2 * k + h]

    sides = (y_near, y_far)
    own_copies = []
    for h, own in ((0, own_a), (1, own_b)):
        for j in [0] + order:
            arrived(own.at[away(-j), 1 - y_hi], fy_sem.at[h, j])
        part = pl.ds(halves[h] * half_rows, half_rows)
        for p in range(public):
            kv_all[blocks + public * s + p, part] = own[chosen_ref[p]]
        own_copies.append(
            pltpu.make_async_copy(own, kv_all.at[pl.ds(0, blocks), part], local_sem.at[2 + h])
        )
        own_copies[-1].start()
        region = unit(s, h)
        send(region, region, x_arrival(1, h), x_next)
        send(region, region, x_arrival(2, h), x_last)
        send(region, region, y_arrival(0, h), sides[h])
        send(region, region, core_arrival(0, 0, h), core_peer)
    for h in range(2):
        for k, onward in ((1, x_next), (2, x_last)):
            region = unit(at_x(steps[k]), h)
            arrived(region, x_arrival(k, h))
            if h == k - 1:
                send(region, region, x_arrival(3, h), onward)
            send(region, region, y_arrival(k, h), sides[h])
            send(region, region, core_arrival(0, k, h), core_peer)
    for h in range(2):
        region = unit(at_x(2), h)
        arrived(region, x_arrival(3, h))
        send(region, region, y_arrival(3, h), sides[h])
        send(region, region, core_arrival(0, 3, h), core_peer)
    for k in range(4):
        for h in range(2):
            region = unit(at_x(steps[k]) + 2 - 4 * y_lo, h)
            arrived(region, y_arrival(k, h))
            send(region, region, core_arrival(1, k, h), core_peer)
    for column in range(2):
        for k in range(4):
            where = at_x(steps[k]) + column * (2 - 4 * y_lo) + 1 - 2 * core
            for h in range(2):
                arrived(unit(where, h), core_arrival(column, k, h))
    for copy in own_copies:
        copy.wait()
    query_local.wait()
    for j in order:
        arrived(q_all.at[away(-j)], q_sem.at[j])

    tall = SHARE * ROWS
    row = lax.broadcasted_iota(jnp.int32, (tall, BLOCK), 0) % ROWS + r * ROWS
    col = lax.broadcasted_iota(jnp.int32, (tall, BLOCK), 1)
    causal = row >= col
    mine = pl.ds(pl.multiple_of(g * wide, wide), wide)
    base = len(pending)

    def offset(j):
        return (1 - 2 * (j % 2)) * (heads // 2 - (j + 1) // 2)

    def home(j):
        return pltpu.make_async_remote_copy(
            src_ref=out_buf.at[j],
            dst_ref=o_ref.at[:, mine],
            send_sem=send_sem.at[base + j],
            recv_sem=o_sem.at[j],
            device_id=across(offset(j)),
            device_id_type=MESH,
        )

    def one_block(j, _):
        b = away(offset(j))
        q = jnp.concatenate([q_all[b, :, h * HD : (h + 1) * HD] for h in range(SHARE)], axis=0)
        carry = attend(q, kv_all[b].reshape(BLOCK, 2 * HD), causal, None, None)

        @pl.when(j > 0)
        def _():
            home(j - 1).start()

        for slot in range(3):
            kv = kv_all[place_ref[b * 3 + slot]].reshape(BLOCK, 2 * HD)
            carry = attend(q, kv, None, bias_ref[b * 3 + slot], carry)
        out = (carry[2] / carry[1]).astype(jnp.bfloat16)
        for h in range(SHARE):
            out_buf[j, :, h * HD : (h + 1) * HD] = out[h * ROWS : (h + 1) * ROWS]
        return 0

    lax.fori_loop(0, heads, one_block, 0)
    last = pltpu.make_async_copy(out_buf.at[heads - 1], o_ref.at[:, mine], local_sem.at[4])
    last.start()
    for copy in pending:
        copy.wait_send()
    for j in range(heads - 1):
        columns = pl.ds(pl.multiple_of(away(-offset(j)) * wide, wide), wide)
        arrived(o_ref.at[:, columns], o_sem.at[j])
        home(j).wait_send()
    last.wait()


def local(queries, key_states, value_states, key_picks, positions):
    local_rows = queries.shape[0]
    kv_heads = key_states.shape[1] // HD

    angles = positions.astype(jnp.float32)[:, None] * frequency_table(HD)[None, :]
    cosine = jnp.cos(angles)
    sine = jnp.sin(angles)
    cosine = jnp.concatenate([cosine, cosine], axis=1)
    sine = jnp.concatenate([-sine, sine], axis=1)

    groups = lax.axis_size("seq")
    all_blocks, picks = key_picks.shape
    blocks = all_blocks // groups
    first_block = lax.axis_index("seq") * blocks
    public = min(picks, blocks)
    block_ids = jnp.arange(all_blocks, dtype=jnp.int32)
    block_group = block_ids // blocks
    picked_later = (key_picks[:, :, None] == block_ids[None, None, :]) & (
        block_group[:, None, None] > block_group[None, None, :]
    )
    is_public = jnp.any(picked_later, axis=(0, 1))
    slot_rank = (
        jnp.cumsum(is_public.reshape(-1, blocks).astype(jnp.int32), axis=1) - 1
    ).reshape(-1)
    place = block_group * public + slot_rank
    own_public = lax.dynamic_slice_in_dim(is_public, first_block, blocks, 0)
    own_rank = lax.dynamic_slice_in_dim(slot_rank, first_block, blocks, 0)
    slot_ids = jnp.arange(public, dtype=jnp.int32)
    chosen = jnp.sum(
        jnp.where(
            own_public[None, :] & (own_rank[None, :] == slot_ids[:, None]),
            jnp.arange(blocks, dtype=jnp.int32)[None, :],
            0,
        ),
        axis=1,
    )
    own_picks = lax.dynamic_slice_in_dim(key_picks, first_block, blocks, 0)
    row_block = first_block + jnp.arange(blocks, dtype=jnp.int32)[:, None]
    near = (own_picks >= first_block) & (own_picks < row_block)
    far = own_picks < first_block
    pick_place = jnp.sum(
        jnp.where(own_picks[:, :, None] == block_ids[None, None, :], place[None, None, :], 0),
        axis=2,
    )
    held = jnp.where(near, own_picks - first_block, jnp.where(far, blocks + pick_place, 0))
    bias = jnp.where(near | far, 0.0, LOWEST).astype(jnp.float32)

    smem = pl.BlockSpec(memory_space=pltpu.SMEM)
    vmem = pl.BlockSpec(memory_space=pltpu.VMEM)
    anywhere = pl.BlockSpec(memory_space=pl.ANY)
    copies = 2 * (kv_heads - 1) + 3 * kv_heads + 30 + (kv_heads - 1)
    return pl.pallas_call(
        functools.partial(group_kernel, blocks, public, groups // 4),
        out_shape=jax.ShapeDtypeStruct(queries.shape, jnp.bfloat16),
        in_specs=[smem, smem, smem, vmem, vmem, vmem, vmem, anywhere],
        out_specs=anywhere,
        scratch_shapes=[
            pltpu.VMEM((kv_heads, local_rows, 2 * HD), jnp.bfloat16),
            pltpu.VMEM(queries.shape, jnp.bfloat16),
            pltpu.VMEM((blocks, SHARE // 2, ROWS, 2 * HD), jnp.bfloat16),
            pltpu.VMEM((blocks, SHARE // 2, ROWS, 2 * HD), jnp.bfloat16),
            pltpu.VMEM((blocks + groups * public, SHARE, ROWS, 2 * HD), jnp.bfloat16),
            pltpu.VMEM((blocks, ROWS, SHARE * HD), jnp.bfloat16),
            pltpu.VMEM((blocks, ROWS, SHARE * HD), jnp.bfloat16),
            pltpu.SemaphoreType.DMA((copies,)),
            pltpu.SemaphoreType.DMA((kv_heads,)),
            pltpu.SemaphoreType.DMA((2, kv_heads)),
            pltpu.SemaphoreType.DMA((kv_heads,)),
            pltpu.SemaphoreType.DMA((kv_heads,)),
            pltpu.SemaphoreType.DMA((30,)),
            pltpu.SemaphoreType.DMA((kv_heads,)),
            pltpu.SemaphoreType.DMA((6,)),
        ],
        compiler_params=pltpu.CompilerParams(
            collective_id=0, has_side_effects=True, vmem_limit_bytes=48 << 20
        ),
        name="group_attention",
    )(chosen, held.reshape(-1), bias.reshape(-1), cosine, sine, key_states, value_states, queries)


def solution(mesh):
    in_specs = (
        P(("seq", "head"), None),
        P(("seq", "head"), None),
        P(("seq", "head"), None),
        P(),
        P(("seq", "head")),
    )
    out_specs = P(("seq", "head"), None)
    return jax.shard_map(local, mesh=mesh, in_specs=in_specs, out_specs=out_specs, check_vma=False)
```

```python
import functools
import math

import jax
import jax.numpy as jnp
from jax import lax
from jax.experimental import pallas as pl
from jax.experimental.pallas import tpu as pltpu
from jax.sharding import PartitionSpec as P

HD = 128
BLOCK = 512
SHARE = 4
ROWS = BLOCK // SHARE
LOWEST = -1e30
SCALE = 1.0 / math.sqrt(HD)
MESH = pl.DeviceIdType.MESH
LOG2E = math.log2(math.e)


def frequency_table(columns):
    inverse = 1.0 / 500000.0 ** (jnp.arange(0, columns, 2, dtype=jnp.float32) / columns)
    wavelength = 2.0 * math.pi / inverse
    smooth = (8192.0 / wavelength - 1.0) / 3.0
    blended = (1.0 - smooth) * inverse / 8.0 + smooth * inverse
    return jnp.where(
        wavelength < 2048.0, inverse, jnp.where(wavelength > 8192.0, inverse / 8.0, blended)
    )


def turn(x, cosine, sine):
    x = x.astype(jnp.float32)
    return (x * cosine + pltpu.roll(x, HD // 2, 1) * sine).astype(jnp.bfloat16)


def attend(q, kv, mask, bias, carry):
    s = lax.dot_general(
        q, kv[:, :HD], (((1,), (1,)), ((), ())), preferred_element_type=jnp.float32
    ) * (SCALE * LOG2E)
    if mask is not None:
        s = jnp.where(mask, s, LOWEST)
    if bias is not None:
        s = s + bias
    top = jnp.max(s, axis=1, keepdims=True)
    if carry is not None:
        top = jnp.maximum(carry[0], top)
    p = jnp.exp2(s - top)
    total = jnp.sum(p, axis=1, keepdims=True)
    product = jnp.dot(p.astype(jnp.bfloat16), kv[:, HD:], preferred_element_type=jnp.float32)
    if carry is not None:
        keep = jnp.exp2(carry[0] - top)
        total = total + carry[1] * keep
        product = product + carry[2] * keep
    return top, total, product


def group_kernel(
    blocks,
    public,
    ring,
    chosen_ref,
    place_ref,
    bias_ref,
    cos_ref,
    sin_ref,
    k_ref,
    v_ref,
    q_ref,
    o_ref,
    kv_in,
    q_in,
    own_a,
    own_b,
    kv_all,
    q_all,
    out_buf,
    send_sem,
    kv_sem,
    fy_sem,
    fz_sem,
    q_sem,
    ag_sem,
    o_sem,
    local_sem,
):
    s = lax.axis_index("seq")
    d = lax.axis_index("head")
    g, r = d // SHARE, d % SHARE
    x, y_lo, core = s // 4, (s // 2) % 2, s % 2
    z_par, y_hi = r // 2, r % 2
    wide = SHARE * HD
    heads = blocks

    def at_x(step):
        return ((x + step + ring) % ring) * 4 + s % 4

    def across(step):
        return (s, ((g + step + heads) % heads) * SHARE + r)

    y_flip = d + 1 - 2 * y_hi
    y_peer = (s, y_flip)
    z_peer = (s, d + 2 - 4 * z_par)
    s_flip = s + 2 - 4 * y_lo
    y_near, y_far = (s_flip, d), (s_flip, y_flip)
    core_peer = (s + 1 - 2 * core, d)
    x_next, x_last = (at_x(1), d), (at_x(-1), d)
    partners = [across(j) for j in range(1, heads)]
    partners += [y_peer, z_peer, y_near, y_far, core_peer, x_next, x_last]

    barrier = pltpu.get_barrier_semaphore()
    for peer in partners:
        pl.semaphore_signal(barrier, inc=1, device_id=peer, device_id_type=MESH)
    raw = pltpu.make_async_copy(q_ref, q_in, local_sem.at[5])
    raw.start()
    for h in range(heads):
        lanes = slice(h * HD, (h + 1) * HD)
        kv_in[h, :, :HD] = turn(k_ref[:, lanes], cos_ref[...], sin_ref[...])
        kv_in[h, :, HD:] = v_ref[:, lanes]
    pl.semaphore_wait(barrier, len(partners))

    pending = []

    def send(source, target, arrival, peer):
        copy = pltpu.make_async_remote_copy(
            src_ref=source,
            dst_ref=target,
            send_sem=send_sem.at[len(pending)],
            recv_sem=arrival,
            device_id=peer,
            device_id_type=MESH,
        )
        copy.start()
        pending.append(copy)

    def arrived(region, arrival):
        pltpu.make_async_remote_copy(
            src_ref=region,
            dst_ref=region,
            send_sem=send_sem.at[0],
            recv_sem=arrival,
            device_id=core_peer,
            device_id_type=MESH,
        ).wait_recv()

    def away(step):
        return (g + step + heads) % heads

    order = []
    for j in range(1, heads // 2 + 1):
        order += [j] if 2 * j == heads else [j, heads - j]

    own_local = pltpu.make_async_copy(kv_in.at[g], own_a.at[g, y_hi], local_sem.at[0])
    own_local.start()
    for j in order:
        send(kv_in.at[away(j)], own_a.at[g, y_hi], kv_sem.at[j], across(j))
    raw.wait()
    for h in range(heads * SHARE):
        lanes = slice(h * HD, (h + 1) * HD)
        q_in[:, lanes] = turn(q_in[:, lanes], cos_ref[...], sin_ref[...])
    query_local = pltpu.make_async_copy(
        q_in.at[:, pl.ds(pl.multiple_of(g * wide, wide), wide)], q_all.at[g], local_sem.at[1]
    )
    query_local.start()
    for j in [0] + order:
        region = own_a.at[away(-j), y_hi]
        if j == 0:
            own_local.wait()
        else:
            arrived(region, kv_sem.at[j])
        send(region, own_b.at[away(-j), y_hi], fz_sem.at[j], z_peer)
        send(region, region, fy_sem.at[0, j], y_peer)
    for j in [0] + order:
        region = own_b.at[away(-j), y_hi]
        arrived(region, fz_sem.at[j])
        send(region, region, fy_sem.at[1, j], y_peer)
    for j in order[::-1]:
        send(
            q_in.at[:, pl.ds(pl.multiple_of(away(j) * wide, wide), wide)],
            q_all.at[g],
            q_sem.at[j],
            across(j),
        )

    half_rows = SHARE // 2
    halves = (z_par, 1 - z_par)
    steps = (0, -1, 1, 2)

    def unit(where, h):
        rows = pl.ds(blocks + public * where, public)
        return kv_all.at[rows, pl.ds(halves[h] * half_rows, half_rows)]

    def x_arrival(k, h):
        return ag_sem.at[2 * (k - 1) + h]

    def y_arrival(k, h):
        return ag_sem.at[6 + 2 * k + h]

    def core_arrival(column, k, h):
        return ag_sem.at[14 + 8 * column + 2 * k + h]

    sides = (y_near, y_far)
    own_copies = []
    for h, own in ((0, own_a), (1, own_b)):
        for j in [0] + order:
            arrived(own.at[away(-j), 1 - y_hi], fy_sem.at[h, j])
        part = pl.ds(halves[h] * half_rows, half_rows)
        for p in range(public):
            kv_all[blocks + public * s + p, part] = own[chosen_ref[p]]
        own_copies.append(
            pltpu.make_async_copy(own, kv_all.at[pl.ds(0, blocks), part], local_sem.at[2 + h])
        )
        own_copies[-1].start()
        region = unit(s, h)
        send(region, region, x_arrival(1, h), x_next)
        send(region, region, x_arrival(2, h), x_last)
        send(region, region, y_arrival(0, h), sides[h])
        send(region, region, core_arrival(0, 0, h), core_peer)
    for h in range(2):
        for k, onward in ((1, x_next), (2, x_last)):
            region = unit(at_x(steps[k]), h)
            arrived(region, x_arrival(k, h))
            if h == k - 1:
                send(region, region, x_arrival(3, h), onward)
            send(region, region, y_arrival(k, h), sides[h])
            send(region, region, core_arrival(0, k, h), core_peer)
    for h in range(2):
        region = unit(at_x(2), h)
        arrived(region, x_arrival(3, h))
        send(region, region, y_arrival(3, h), sides[h])
        send(region, region, core_arrival(0, 3, h), core_peer)
    for k in range(4):
        for h in range(2):
            region = unit(at_x(steps[k]) + 2 - 4 * y_lo, h)
            arrived(region, y_arrival(k, h))
            send(region, region, core_arrival(1, k, h), core_peer)
    for column in range(2):
        for k in range(4):
            where = at_x(steps[k]) + column * (2 - 4 * y_lo) + 1 - 2 * core
            for h in range(2):
                arrived(unit(where, h), core_arrival(column, k, h))
    for copy in own_copies:
        copy.wait()
    query_local.wait()
    for j in order:
        arrived(q_all.at[away(-j)], q_sem.at[j])

    tall = SHARE * ROWS
    row = lax.broadcasted_iota(jnp.int32, (tall, BLOCK), 0) % ROWS + r * ROWS
    col = lax.broadcasted_iota(jnp.int32, (tall, BLOCK), 1)
    causal = row >= col
    mine = pl.ds(pl.multiple_of(g * wide, wide), wide)
    base = len(pending)

    def offset(j):
        return (1 - 2 * (j % 2)) * (heads // 2 - (j + 1) // 2)

    def home(j):
        return pltpu.make_async_remote_copy(
            src_ref=out_buf.at[j],
            dst_ref=o_ref.at[:, mine],
            send_sem=send_sem.at[base + j],
            recv_sem=o_sem.at[j],
            device_id=across(offset(j)),
            device_id_type=MESH,
        )

    def one_block(j, _):
        b = away(offset(j))
        q = jnp.concatenate([q_all[b, :, h * HD : (h + 1) * HD] for h in range(SHARE)], axis=0)
        carry = attend(q, kv_all[b].reshape(BLOCK, 2 * HD), causal, None, None)

        @pl.when(j > 0)
        def _():
            home(j - 1).start()

        for slot in range(3):
            kv = kv_all[place_ref[b * 3 + slot]].reshape(BLOCK, 2 * HD)
            carry = attend(q, kv, None, bias_ref[b * 3 + slot], carry)
        out = (carry[2] / carry[1]).astype(jnp.bfloat16)
        for h in range(SHARE):
            out_buf[j, :, h * HD : (h + 1) * HD] = out[h * ROWS : (h + 1) * ROWS]
        return 0

    lax.fori_loop(0, heads, one_block, 0)
    last = pltpu.make_async_copy(out_buf.at[heads - 1], o_ref.at[:, mine], local_sem.at[4])
    last.start()
    for copy in pending:
        copy.wait_send()
    for j in range(heads - 1):
        columns = pl.ds(pl.multiple_of(away(-offset(j)) * wide, wide), wide)
        arrived(o_ref.at[:, columns], o_sem.at[j])
        home(j).wait_send()
    last.wait()


def local(queries, key_states, value_states, key_picks, positions):
    local_rows = queries.shape[0]
    kv_heads = key_states.shape[1] // HD

    angles = positions.astype(jnp.float32)[:, None] * frequency_table(HD)[None, :]
    cosine = jnp.cos(angles)
    sine = jnp.sin(angles)
    cosine = jnp.concatenate([cosine, cosine], axis=1)
    sine = jnp.concatenate([-sine, sine], axis=1)

    groups = lax.axis_size("seq")
    all_blocks, picks = key_picks.shape
    blocks = all_blocks // groups
    first_block = lax.axis_index("seq") * blocks
    public = min(picks, blocks)
    block_ids = jnp.arange(all_blocks, dtype=jnp.int32)
    block_group = block_ids // blocks
    picked_later = (key_picks[:, :, None] == block_ids[None, None, :]) & (
        block_group[:, None, None] > block_group[None, None, :]
    )
    is_public = jnp.any(picked_later, axis=(0, 1))
    slot_rank = (
        jnp.cumsum(is_public.reshape(-1, blocks).astype(jnp.int32), axis=1) - 1
    ).reshape(-1)
    place = block_group * public + slot_rank
    own_public = lax.dynamic_slice_in_dim(is_public, first_block, blocks, 0)
    own_rank = lax.dynamic_slice_in_dim(slot_rank, first_block, blocks, 0)
    slot_ids = jnp.arange(public, dtype=jnp.int32)
    chosen = jnp.sum(
        jnp.where(
            own_public[None, :] & (own_rank[None, :] == slot_ids[:, None]),
            jnp.arange(blocks, dtype=jnp.int32)[None, :],
            0,
        ),
        axis=1,
    )
    own_picks = lax.dynamic_slice_in_dim(key_picks, first_block, blocks, 0)
    row_block = first_block + jnp.arange(blocks, dtype=jnp.int32)[:, None]
    near = (own_picks >= first_block) & (own_picks < row_block)
    far = own_picks < first_block
    pick_place = jnp.sum(
        jnp.where(own_picks[:, :, None] == block_ids[None, None, :], place[None, None, :], 0),
        axis=2,
    )
    held = jnp.where(near, own_picks - first_block, jnp.where(far, blocks + pick_place, 0))
    bias = jnp.where(near | far, 0.0, LOWEST).astype(jnp.float32)

    smem = pl.BlockSpec(memory_space=pltpu.SMEM)
    vmem = pl.BlockSpec(memory_space=pltpu.VMEM)
    anywhere = pl.BlockSpec(memory_space=pl.ANY)
    copies = 2 * (kv_heads - 1) + 3 * kv_heads + 30 + (kv_heads - 1)
    return pl.pallas_call(
        functools.partial(group_kernel, blocks, public, groups // 4),
        out_shape=jax.ShapeDtypeStruct(queries.shape, jnp.bfloat16),
        in_specs=[smem, smem, smem, vmem, vmem, vmem, vmem, anywhere],
        out_specs=anywhere,
        scratch_shapes=[
            pltpu.VMEM((kv_heads, local_rows, 2 * HD), jnp.bfloat16),
            pltpu.VMEM(queries.shape, jnp.bfloat16),
            pltpu.VMEM((blocks, SHARE // 2, ROWS, 2 * HD), jnp.bfloat16),
            pltpu.VMEM((blocks, SHARE // 2, ROWS, 2 * HD), jnp.bfloat16),
            pltpu.VMEM((blocks + groups * public, SHARE, ROWS, 2 * HD), jnp.bfloat16),
            pltpu.VMEM((blocks, ROWS, SHARE * HD), jnp.bfloat16),
            pltpu.VMEM((blocks, ROWS, SHARE * HD), jnp.bfloat16),
            pltpu.SemaphoreType.DMA((copies,)),
            pltpu.SemaphoreType.DMA((kv_heads,)),
            pltpu.SemaphoreType.DMA((2, kv_heads)),
            pltpu.SemaphoreType.DMA((kv_heads,)),
            pltpu.SemaphoreType.DMA((kv_heads,)),
            pltpu.SemaphoreType.DMA((30,)),
            pltpu.SemaphoreType.DMA((kv_heads,)),
            pltpu.SemaphoreType.DMA((6,)),
        ],
        compiler_params=pltpu.CompilerParams(
            collective_id=0, has_side_effects=True, vmem_limit_bytes=48 << 20
        ),
        name="group_attention",
    )(chosen, held.reshape(-1), bias.reshape(-1), cosine, sine, key_states, value_states, queries)


def solution(mesh):
    in_specs = (
        P(("seq", "head"), None),
        P(("seq", "head"), None),
        P(("seq", "head"), None),
        P(),
        P(("seq", "head")),
    )
    out_specs = P(("seq", "head"), None)
    return jax.shard_map(local, mesh=mesh, in_specs=in_specs, out_specs=out_specs, check_vma=False)
```
